512 devices in a mesh: dp: 64 (over z, x_lo, core), seq: 8 (over x_hi, y).
Axes of the slice: x: 4 (x_hi: 2, x_lo: 2; x = x_hi * 2 + x_lo), y: 4, z: 16, core: 2. Of those that a mesh axis runs over, the one named last changes fastest.
Arguments:
- queries: bfloat16 [65536, 3072], P(('dp', 'seq')), may hold values from -6 to 6
- key_states: bfloat16 [65536, 3072], P(('dp', 'seq')), may hold values from -6 to 6
- value_states: bfloat16 [65536, 3072], P(('dp', 'seq')), may hold values from -6 to 6
- grad_out: bfloat16 [65536, 2560], P(('dp', 'seq')), may hold values from -24 to 24
- out_weight: bfloat16 [3072, 2560], P('seq', 'dp'), may hold values from -0.109375 to 0.109375
- key_blocks: int32 [24, 16, 16], replicated, may hold values from 0 to 15, as said below
- key_count: int32 [24, 16], replicated, may hold values from 5 to 16
Outputs:
- grad_queries: bfloat16 [65536, 3072], P(('dp', 'seq'))
- grad_keys: bfloat16 [65536, 3072], P(('dp', 'seq'))
- grad_weight: float32 [3072, 2560], P('seq', 'dp')
The draws below stay inside these ranges and needn't reach their ends.
Inputs may be any that keep to these rules, and one draw needn't show every extreme that they name: The first key_count[h, b] entries of key_blocks[h, b] name distinct key blocks; later entries name the other blocks and are not used. Query blocks 0 and 15 attend all 16 blocks; every other query block attends at most 8 blocks, and some reach 8 for every head.
All inputs are finite; a program needn't handle non-finite values.
Results may differ from the reference program's by a relative error of at most 0.0079.
Values may be sent and summed in bfloat16 or wider, within the bound.
A program may use at most 64 MiB of HBM per device.

```python
import jax
import jax.numpy as jnp
from jax import lax

HEADS = 24
HD = 128
CW = 2560
BLK = 64
RANDB = 3
LENGTH = 1024
NB = 16
TOKENS = 65536


def base_draw(key, salt):
    shape = (TOKENS, HEADS, HD)
    return jax.random.truncated_normal(jax.random.fold_in(key, salt), -6.0, 6.0, shape, jnp.float32)


def draw_queries(key, part):
    values = base_draw(key, 1)
    return values.reshape(TOKENS, HEADS * HD).astype(jnp.bfloat16)


def draw_key_states(key, part):
    values = base_draw(key, 2)
    return values.reshape(TOKENS, HEADS * HD).astype(jnp.bfloat16)


def layout(key):
    block_total = NB
    column = jnp.arange(block_total)
    block_row = jnp.arange(block_total)
    global_row = (block_row == 0) | (block_row == block_total - 1)
    mandatory = (column[None, :] == 0) | (column[None, :] == block_total - 1)
    mandatory = mandatory | (jnp.abs(column[None, :] - block_row[:, None]) <= 1) | global_row[:, None]
    extra = jax.random.randint(jax.random.fold_in(key, 21), (HEADS, block_total), 1, RANDB + 1)
    extra = jnp.where((block_row == block_total // 2)[None, :], RANDB, extra)
    counted = jnp.sum(mandatory.astype(jnp.int32), axis=-1)
    count_out = jnp.minimum(counted[None, :] + extra, block_total)
    noise = jax.random.randint(jax.random.fold_in(key, 22), (HEADS, block_total, block_total), 0, 4096)
    priority = jnp.where(mandatory[None], 1 << 24, 0) + noise * block_total + column[None, None, :]
    order = lax.top_k(priority, block_total)[1]
    return (order.astype(jnp.int32), count_out.astype(jnp.int32))


def draw_key_blocks(key, part):
    return layout(key)[0]


def draw_key_count(key, part):
    return layout(key)[1]


def spiked(result, own_key, source, target, shards_of, factor):
    def block_of(dim):
        return (jnp.arange(result.shape[dim]) // (result.shape[dim] // shards_of)).reshape((-1,) + (1,) * (result.ndim - 1 - dim))

    first = jax.random.permutation(own_key, shards_of)[block_of(target)]
    far = (block_of(target) + shards_of // 2) % shards_of
    return jnp.where((block_of(source) == first) | (block_of(source) == far), factor * result, result)


def shard_levels(stream_key, dims, split, least, largest):
    def one(dim, parts):
        heights = jax.random.uniform(jax.random.fold_in(jax.random.fold_in(stream_key, 6), dim), (parts,), jnp.float32, least / len(split), largest / len(split))
        return jnp.repeat(jnp.exp(heights), dims[dim] // parts).reshape((-1,) + (1,) * (len(dims) - dim - 1))

    level = one(*split[0])
    for cut in split[1:]:
        level = level * one(*cut)
    return level


def normal_values(rng, shape, scale, most, pieces=(), kind=jnp.bfloat16):
    values = scale * jax.random.normal(rng, shape, jnp.float32)
    if pieces:
        values = values * shard_levels(rng, shape, pieces, -0.22, 0.18)
    return jnp.clip(values, -most, most).astype(kind)


def noise_with(stream_key, dims, scale, limit, split, heavy, kind=jnp.bfloat16):
    result = scale * jax.random.normal(stream_key, dims, jnp.float32)
    if split:
        result = result * shard_levels(stream_key, dims, split, -0.22, 0.18)
    return jnp.clip(spiked(result, jax.random.fold_in(stream_key, 3), *heavy), -limit, limit).astype(kind)


def setup_inputs(seed: int = 0) -> dict:
    key_list = jax.random.split(jax.random.key(seed), 8)
    queries = draw_queries(jax.random.fold_in(key_list[7], 71), 0)
    key_states = draw_key_states(jax.random.fold_in(key_list[7], 71), 0)
    value_states = normal_values(key_list[2], (TOKENS, HEADS * HD), 1.0, 6.0, ((0, 512),))
    grad_out = noise_with(key_list[3], (TOKENS, CW), 1.0, 24.0, ((0, 512),), (0, 1, 512, 6.0))
    out_weight = normal_values(key_list[4], (HEADS * HD, CW), (HEADS * HD) ** -0.5, 0.109375, ((0, 8), (1, 64)))
    key_blocks = draw_key_blocks(jax.random.fold_in(key_list[7], 71), 0)
    key_count = draw_key_count(jax.random.fold_in(key_list[7], 71), 0)
    return {"queries": queries, "key_states": key_states, "value_states": value_states, "grad_out": grad_out, "out_weight": out_weight, "key_blocks": key_blocks, "key_count": key_count}


def reference(queries, key_states, value_states, grad_out, out_weight, key_blocks, key_count):
    block_total = LENGTH // BLK
    live_slots = jnp.arange(block_total)[None, None, :] < key_count[:, :, None]
    hits = (key_blocks[:, :, :, None] == jnp.arange(block_total)[None, None, None, :]) & live_slots[:, :, :, None]
    allowed = jnp.any(hits, axis=2)
    token_mask = jnp.repeat(jnp.repeat(allowed, BLK, axis=1), BLK, axis=2)
    weight_heads = out_weight.astype(jnp.float32).reshape(HEADS, HD, CW)
    scale = HD ** -0.5
    seq_total = TOKENS // LENGTH

    def split_heads(array_in):
        return array_in.astype(jnp.float32).reshape(LENGTH, HEADS, HD).transpose(1, 0, 2)

    def merge_heads(array_in):
        return array_in.transpose(1, 0, 2).reshape(LENGTH, HEADS * HD)

    def one_sequence(running_sum, inputs):
        query_seq, key_seq, value_seq, grad_seq = inputs
        query_f = split_heads(query_seq)
        key_f = split_heads(key_seq)
        value_f = split_heads(value_seq)
        grad_f = grad_seq.astype(jnp.float32)
        scores = jnp.einsum("hid,hjd->hij", query_f, key_f) * scale
        scores = jnp.where(token_mask, scores, -jnp.inf)
        row_max = jnp.max(scores, axis=-1, keepdims=True)
        expo = jnp.exp(scores - row_max)
        probs = expo / jnp.sum(expo, axis=-1, keepdims=True)
        probs_b = lax.optimization_barrier(probs.astype(jnp.bfloat16)).astype(jnp.float32)
        head_outputs = jnp.einsum("hij,hjd->hid", probs_b, value_f).astype(jnp.bfloat16)
        grad_heads = jnp.einsum("lc,hdc->hld", grad_f, weight_heads).astype(jnp.bfloat16)
        grad_heads = lax.optimization_barrier(grad_heads).astype(jnp.float32)
        dprob = jnp.einsum("hid,hjd->hij", grad_heads, value_f)
        row_delta = jnp.sum(probs * dprob, axis=-1, keepdims=True)
        dscore = (probs * (dprob - row_delta) * scale).astype(jnp.bfloat16)
        dscore = lax.optimization_barrier(dscore).astype(jnp.float32)
        grad_q = jnp.einsum("hij,hjd->hid", dscore, key_f).astype(jnp.bfloat16)
        grad_k = jnp.einsum("hij,hid->hjd", dscore, query_f).astype(jnp.bfloat16)
        outs_f = lax.optimization_barrier(head_outputs).astype(jnp.float32)
        running_sum = running_sum + jnp.einsum("hld,lc->hdc", outs_f, grad_f).reshape(HEADS * HD, CW)
        return running_sum, (merge_heads(grad_q), merge_heads(grad_k))

    inputs = (queries.reshape(seq_total, LENGTH, HEADS * HD),
              key_states.reshape(seq_total, LENGTH, HEADS * HD),
              value_states.reshape(seq_total, LENGTH, HEADS * HD),
              grad_out.reshape(seq_total, LENGTH, CW))
    start_sum = jnp.zeros((HEADS * HD, CW), jnp.float32)
    grad_weight, (grad_queries, grad_keys) = lax.scan(one_sequence, start_sum, inputs)
    return grad_queries.reshape(TOKENS, HEADS * HD), grad_keys.reshape(TOKENS, HEADS * HD), grad_weight
```

```python
import functools

import jax
import jax.numpy as jnp
from jax import lax
from jax.experimental import pallas as pl
from jax.experimental.pallas import tpu as pltpu
from jax.sharding import PartitionSpec as P

HEADS = 24
HD = 128
BLK = 64
LOG2E = 1.4426950408889634
MESH = pl.DeviceIdType.MESH

SEQ = 8
ROWS = 128
LEN = SEQ * ROWS
LH = HEADS // SEQ
LW = LH * HD
CW = 2560
HALF = ROWS // 2
ZN = 16
OWN = CW // 64


def dot_nn(a, b):
    return lax.dot_general(a, b, (((1,), (0,)), ((), ())), preferred_element_type=jnp.float32)


def dot_nt(a, b):
    return lax.dot_general(a, b, (((1,), (1,)), ((), ())), preferred_element_type=jnp.float32)


def dot_tn(a, b):
    return lax.dot_general(a, b, (((0,), (0,)), ((), ())), preferred_element_type=jnp.float32)


def kernel(
    q_ref, k_ref, v_ref, g_ref, w_ref, kb_ref,
    dq_out, dk_out, dw_out,
    qg, kg, vg, gall, wbuf, wt, bias, probs, outs, dqb, dkb, dkacc, gw,
    rsrc, r1, t1, r2, t2, r3,
    in_send, in_recv, loc, g_send, g_recv, w_send, w_recv, o_send, o_recv, r_send, r_recv,
):
    dp = lax.axis_index("dp")
    me = lax.axis_index("seq")
    z = dp // 4
    quad = dp % 4
    xl = quad // 2
    core = quad % 2
    xh = me // 4
    y = me % 4

    def seq_at(dx, dy):
        return ((xh + dx) % 2) * 4 + (y + dy) % 4

    peers = [seq_at(dx, dy) for dx, dy in ((0, 1), (0, 3), (1, 0), (0, 2), (1, 1), (1, 3), (1, 2))]
    mate = z * 4 + xl * 2 + (1 - core)
    side = z * 4 + (1 - xl) * 2 + core

    def z_at(d):
        return (z + d) % ZN

    barrier = pltpu.get_barrier_semaphore()
    targets = [(dp, p) for p in peers] + [(mate, me), (side, me)]
    targets += [(z_at(d) * 4 + quad, me) for d in range(1, ZN)]
    for t in targets:
        pl.semaphore_signal(barrier, inc=1, device_id=t, device_id_type=MESH)

    def cols(p):
        return pl.ds(pl.multiple_of(p * LW, 128), LW)

    local = [
        pltpu.make_async_copy(src.at[:, cols(me)], dst.at[me], loc.at[i])
        for i, (src, dst) in enumerate(((q_ref, qg), (k_ref, kg), (v_ref, vg)))
    ]
    local.append(pltpu.make_async_copy(g_ref, gall.at[me], loc.at[3]))
    local.append(pltpu.make_async_copy(w_ref, wbuf.at[quad, z], loc.at[4]))
    for c in local:
        c.start()

    key_block = lax.broadcasted_iota(jnp.int32, (16, LEN), 1) // BLK
    for h in range(LH):
        lists = kb_ref[me * LH + h]
        hit = key_block == lists[:, 0:1]
        for s in range(1, 16):
            hit = hit | (key_block == lists[:, s : s + 1])
        row = jnp.where(hit, 0.0, -jnp.inf).astype(jnp.float32)
        for s in range(SEQ):
            bias[h, s] = row[2 * s : 2 * s + 2]

    pl.semaphore_wait(barrier, len(targets))

    def remote(src, dst, ssem, rsem, dev):
        return pltpu.make_async_remote_copy(
            src_ref=src, dst_ref=dst, send_sem=ssem, recv_sem=rsem, device_id=dev, device_id_type=MESH
        )

    in_copies = []
    for a, (src, dst) in enumerate(((q_ref, qg), (k_ref, kg), (v_ref, vg))):
        for i, p in enumerate(peers):
            n = a * 7 + i
            in_copies.append(remote(src.at[:, cols(p)], dst.at[me], in_send.at[n], in_recv.at[n], (dp, p)))
    for c in in_copies:
        c.start()

    w_copies = []
    for d in range(1, ZN):
        w_copies.append(
            remote(w_ref, wbuf.at[quad, z], w_send.at[d - 1], w_recv.at[d - 1], (z_at(d) * 4 + quad, me))
        )
    for c in w_copies:
        c.start()

    lo, hi = pl.ds(0, HALF), pl.ds(HALF, HALF)
    up, down, across = (dp, seq_at(0, 1)), (dp, seq_at(0, 3)), (dp, seq_at(1, 0))
    order = [(0, 0), (0, 3), (0, 1), (1, 0), (0, 2), (1, 3), (1, 1), (1, 2)]
    slot_of = {o: seq_at(*o) for o in order}

    def sem_of(dx, dy, half):
        return (order.index((dx % 2, dy % 4)) - 1) * 2 + half

    g_copies = {}

    def pass_on(dx, dy, half, way):
        dev, tdx, tdy = {"up": (up, dx, dy - 1), "down": (down, dx, dy + 1), "across": (across, dx + 1, dy)}[way]
        rows = hi if half else lo
        n = sem_of(tdx, tdy, half)
        src = gall.at[slot_of[(dx % 2, dy % 4)], rows]
        if (dx, dy) == (0, 0):
            src = g_ref.at[rows]
        c = remote(src, gall.at[slot_of[(dx % 2, dy % 4)], rows], g_send.at[n], g_recv.at[n], dev)
        c.start()
        g_copies[n] = c

    done = set()

    def arrived(dx, dy, half):
        n = sem_of(dx, dy, half)
        if n not in done:
            done.add(n)
            g_copies[n].wait_recv()

    for half in (0, 1):
        pass_on(0, 0, half, "across")
        pass_on(0, 0, half, "up")
        pass_on(0, 0, half, "down")

    for c in local:
        c.wait()
    for c in in_copies:
        c.wait_recv()

    def head_cols(h):
        return pl.ds(pl.multiple_of(h * HD, HD), HD)

    scale = HD ** -0.5

    def forward(n, carry):
        s = n // LH
        h = n % LH
        hc = head_cols(h)
        query = qg[s, :, hc]
        key = kg[:, :, hc].reshape(LEN, HD)
        value = vg[:, :, hc].reshape(LEN, HD)
        scores = dot_nt(query, key) * (scale * LOG2E)
        b = bias[h, s]
        mask = jnp.concatenate(
            (jnp.broadcast_to(b[0:1], (BLK, LEN)), jnp.broadcast_to(b[1:2], (BLK, LEN))), axis=0
        )
        scores = scores + mask
        expo = jnp.exp2(scores - jnp.max(scores, axis=-1, keepdims=True))
        p = expo * (1.0 / jnp.sum(expo, axis=-1, keepdims=True))
        probs[h, s] = p
        outs[s, :, hc] = dot_nn(p.astype(jnp.bfloat16), value).astype(jnp.bfloat16)
        return carry

    def relay_first():
        arrived(0, 3, 0)
        pass_on(0, 3, 0, "up")
        pass_on(0, 3, 0, "across")
        arrived(0, 1, 1)
        pass_on(0, 1, 1, "down")
        pass_on(0, 1, 1, "across")
        arrived(1, 0, 0)
        pass_on(1, 0, 0, "down")
        arrived(1, 0, 1)
        pass_on(1, 0, 1, "up")

    def relay_second():
        arrived(1, 3, 0)
        pass_on(1, 3, 0, "up")
        arrived(1, 1, 1)
        pass_on(1, 1, 1, "down")

    lax.fori_loop(0, SEQ * LH, forward, 0)

    for c in w_copies:
        c.wait_recv()
    plane_mate = remote(wbuf.at[quad], wbuf.at[quad], w_send.at[15], w_recv.at[15], (mate, me))
    plane_side = remote(wbuf.at[quad], wbuf.at[quad], w_send.at[16], w_recv.at[16], (side, me))
    plane_mate.start()
    plane_side.start()
    relay_first()
    plane_side.wait_recv()
    far = (1 - xl) * 2 + core
    plane_far = remote(wbuf.at[far], wbuf.at[far], w_send.at[17], w_recv.at[17], (mate, me))
    plane_far.start()
    plane_mate.wait_recv()
    plane_far.wait_recv()

    def assemble(i, carry):
        group = jnp.concatenate([wbuf[q, i].astype(jnp.float32) for q in range(4)], axis=0)
        wt[pl.ds(pl.multiple_of(i * 4 * OWN, 32), 4 * OWN), :] = group.astype(jnp.bfloat16)
        return carry

    lax.fori_loop(0, ZN, assemble, 0)

    o_copies = []

    def backward(step):
        slot = slot_of[order[step]]
        grad_heads = dot_nn(gall[slot], wt[...]).astype(jnp.bfloat16)
        dqb[slot] = grad_heads

        def one_head(h, carry):
            hc = head_cols(h)
            key = kg[:, :, hc].reshape(LEN, HD)
            value = vg[:, :, hc].reshape(LEN, HD)
            dprob = dot_nt(dqb[slot, :, hc], value)
            p = probs[h, slot]
            delta = jnp.sum(p * dprob, axis=-1, keepdims=True)
            dscore = (p * (dprob - delta) * scale).astype(jnp.bfloat16)
            dqb[slot, :, hc] = dot_nn(dscore, key).astype(jnp.bfloat16)
            part = dot_tn(dscore, qg[slot, :, hc])
            if step == 0:
                dkacc[h] = part
            else:
                dkacc[h] += part
            return carry

        lax.fori_loop(0, LH, one_head, 0)
        if step == 0:
            c = pltpu.make_async_copy(dqb.at[slot], dq_out.at[:, cols(me)], loc.at[5])
        else:
            c = remote(
                dqb.at[slot], dq_out.at[:, cols(me)], o_send.at[step - 1], o_recv.at[step - 1], (dp, slot)
            )
        c.start()
        o_copies.append(c)

    backward(0)
    for step in range(1, SEQ):
        if step == 1:
            relay_second()
        for half in (0, 1):
            arrived(*order[step], half)
        backward(step)

    def weight_rows(i, carry):
        cc = pl.ds(pl.multiple_of(i * 512, 512), 512)
        part = dot_tn(gall[:, :, cc].reshape(LEN, 512), outs[...].reshape(LEN, LW))
        gw[cc, :] = part
        return carry

    lax.fori_loop(0, CW // 512, weight_rows, 0)

    def spread(i, carry):
        for q in range(4):
            rows = pl.ds(pl.multiple_of(i * 4 * OWN + q * OWN, 8), OWN)
            rsrc[q, i] = gw[rows, :].astype(jnp.bfloat16)
        return carry

    lax.fori_loop(0, ZN, spread, 0)

    other = 1 - core
    pair = [
        remote(rsrc.at[x * 2 + other], r1.at[x], r_send.at[x], r_recv.at[x], (mate, me)) for x in range(2)
    ]
    for c in pair:
        c.start()

    for h in range(LH):
        dkb[:, :, h * HD : (h + 1) * HD] = dkacc[h].astype(jnp.bfloat16).reshape(SEQ, ROWS, HD)
    k_copies = [pltpu.make_async_copy(dkb.at[me], dk_out.at[:, cols(me)], loc.at[6])]
    for step in range(1, SEQ):
        slot = slot_of[order[step]]
        n = 6 + step
        k_copies.append(remote(dkb.at[slot], dk_out.at[:, cols(me)], o_send.at[n], o_recv.at[n], (dp, slot)))
    for c in k_copies:
        c.start()

    for c in pair:
        c.wait_recv()

    def add_side(i, carry):
        t1[i] = (rsrc[(1 - xl) * 2 + core, i].astype(jnp.float32) + r1[1 - xl, i].astype(jnp.float32)).astype(
            jnp.bfloat16
        )
        return carry

    lax.fori_loop(0, ZN, add_side, 0)
    side_copy = remote(t1, r2, r_send.at[2], r_recv.at[2], (side, me))
    side_copy.start()
    side_copy.wait_recv()

    def add_own(i, carry):
        total = rsrc[quad, i].astype(jnp.float32) + r1[xl, i].astype(jnp.float32) + r2[i].astype(jnp.float32)
        t2[i] = total.astype(jnp.bfloat16)
        return carry

    lax.fori_loop(0, ZN, add_own, 0)
    z_copies = []
    for d in range(1, ZN):
        z_copies.append(
            remote(
                t2.at[z_at(d)], r3.at[d - 1], r_send.at[2 + d], r_recv.at[2 + d], (z_at(d) * 4 + quad, me)
            )
        )
    for c in z_copies:
        c.start()
    total = t2[z].astype(jnp.float32)
    for d, c in enumerate(z_copies):
        c.wait_recv()
        total = total + r3[d].astype(jnp.float32)
    dw_out[...] = total

    for c in (o_copies[0], k_copies[0]):
        c.wait()
    for c in o_copies[1:] + k_copies[1:]:
        c.wait()
    for c in in_copies + w_copies + list(g_copies.values()):
        c.wait_send()
    for c in (plane_mate, plane_side, plane_far, pair[0], pair[1], side_copy):
        c.wait_send()
    for c in z_copies:
        c.wait_send()


def per_device(queries, key_states, value_states, grad_out, out_weight, key_blocks, key_count):
    bf, f32 = jnp.bfloat16, jnp.float32
    used = jnp.arange(16)[None, None, :] < key_count[:, :, None]
    lists = jnp.where(used, key_blocks, -1)
    vmem = pl.BlockSpec(memory_space=pltpu.VMEM)
    dma = pltpu.SemaphoreType.DMA
    grad_q, grad_k, grad_w = pl.pallas_call(
        kernel,
        name="bigbird_backward",
        out_shape=(
            jax.ShapeDtypeStruct((ROWS, HEADS * HD), bf),
            jax.ShapeDtypeStruct((ROWS, HEADS * HD), bf),
            jax.ShapeDtypeStruct((OWN, LW), f32),
        ),
        in_specs=[vmem] * 6,
        out_specs=(vmem, vmem, vmem),
        scratch_shapes=[
            pltpu.VMEM((SEQ, ROWS, LW), bf),
            pltpu.VMEM((SEQ, ROWS, LW), bf),
            pltpu.VMEM((SEQ, ROWS, LW), bf),
            pltpu.VMEM((SEQ, ROWS, CW), bf),
            pltpu.VMEM((4, ZN, OWN, LW), bf),
            pltpu.VMEM((CW, LW), bf),
            pltpu.VMEM((LH, SEQ, 2, LEN), f32),
            pltpu.VMEM((LH, SEQ, ROWS, LEN), f32),
            pltpu.VMEM((SEQ, ROWS, LW), bf),
            pltpu.VMEM((SEQ, ROWS, LW), bf),
            pltpu.VMEM((SEQ, ROWS, LW), bf),
            pltpu.VMEM((LH, LEN, HD), f32),
            pltpu.VMEM((CW, LW), f32),
            pltpu.VMEM((4, ZN, OWN, LW), bf),
            pltpu.VMEM((2, ZN, OWN, LW), bf),
            pltpu.VMEM((ZN, OWN, LW), bf),
            pltpu.VMEM((ZN, OWN, LW), bf),
            pltpu.VMEM((ZN, OWN, LW), bf),
            pltpu.VMEM((ZN - 1, OWN, LW), bf),
            dma((21,)), dma((21,)), dma((7,)),
            dma((14,)), dma((14,)),
            dma((18,)), dma((18,)),
            dma((14,)), dma((14,)),
            dma((18,)), dma((18,)),
        ],
        compiler_params=pltpu.CompilerParams(
            collective_id=0, has_side_effects=True, vmem_limit_bytes=60 * 1024 * 1024
        ),
    )(queries, key_states, value_states, grad_out, out_weight.T, lists)
    return grad_q, grad_k, grad_w.T


def solution(mesh):
    return jax.shard_map(
        per_device,
        mesh=mesh,
        in_specs=(
            P(("dp", "seq"), None),
            P(("dp", "seq"), None),
            P(("dp", "seq"), None),
            P(("dp", "seq"), None),
            P("seq", "dp"),
            P(),
            P(),
        ),
        out_specs=(P(("dp", "seq"), None), P(("dp", "seq"), None), P("seq", "dp")),
        check_vma=False,
    )
```

```python
import jax
import jax.numpy as jnp
from jax import lax
from jax.experimental import pallas as pl
from jax.experimental.pallas import tpu as pltpu
from jax.sharding import PartitionSpec as P

HEADS = 24
HD = 128
BLK = 64
NB = 16
LOG2E = 1.4426950408889634
MESH = pl.DeviceIdType.MESH

SEQ = 8
ROWS = 128
LEN = SEQ * ROWS
LH = HEADS // SEQ
LW = LH * HD
CW = 2560
HALF = ROWS // 2
ZN = 16
OWN = CW // 64
TILE = 512
SUB = 16
CHUNK = 512


def dot_nn(a, b):
    return lax.dot_general(a, b, (((1,), (0,)), ((), ())), preferred_element_type=jnp.float32)


def dot_nt(a, b):
    return lax.dot_general(a, b, (((1,), (1,)), ((), ())), preferred_element_type=jnp.float32)


def dot_tn(a, b):
    return lax.dot_general(a, b, (((0,), (0,)), ((), ())), preferred_element_type=jnp.float32)


def remote(src, dst, ssem, rsem, dev):
    return pltpu.make_async_remote_copy(
        src_ref=src, dst_ref=dst, send_sem=ssem, recv_sem=rsem, device_id=dev, device_id_type=MESH
    )


def kernel(
    q_ref, k_ref, v_ref, g_ref, w_ref, kb_ref, kc_ref,
    dq_out, dk_out, dw_out,
    qg, kg, vg, gall, gturn, wbuf, wt, bias, work, expos, half, outs, wide, inverse, gheads, dqb, dkb,
    rsrc, r1, t1, r2, t2, r3,
    in_send, in_recv, loc, g_send, g_recv, w_send, w_recv, o_send, o_recv, r_send, r_recv,
):
    bf, f32 = jnp.bfloat16, jnp.float32
    dp = lax.axis_index("dp")
    me = lax.axis_index("seq")
    z = dp // 4
    quad = dp % 4
    xl = quad // 2
    core = quad % 2
    xh = me // 4
    y = me % 4

    def seq_at(dx, dy):
        return ((xh + dx) % 2) * 4 + (y + dy) % 4

    order = [(0, 0), (0, 3), (0, 1), (1, 0), (0, 2), (1, 3), (1, 1), (1, 2)]
    slot_of = {o: seq_at(*o) for o in order}
    peers = [slot_of[o] for o in order[1:]]
    mate = (z * 4 + xl * 2 + (1 - core), me)
    side = (z * 4 + (1 - xl) * 2 + core, me)
    along_z = [(((z + d) % ZN) * 4 + quad, me) for d in range(1, ZN)]

    barrier = pltpu.get_barrier_semaphore()
    targets = along_z + [(dp, p) for p in peers] + [mate, side]
    for t in targets:
        pl.semaphore_signal(barrier, inc=1, device_id=t, device_id_type=MESH)

    def cols(p, h):
        return pl.ds(pl.multiple_of(p * LW + h * HD, 128), HD)

    inputs = ((q_ref, qg), (k_ref, kg), (v_ref, vg))
    local = [pltpu.make_async_copy(g_ref, gall.at[me], loc.at[0])]
    local.append(pltpu.make_async_copy(w_ref, wbuf.at[quad, z], loc.at[1]))
    for a, (src, dst) in enumerate(inputs):
        for h in range(LH):
            local.append(pltpu.make_async_copy(src.at[:, cols(me, h)], dst.at[h, me], loc.at[2 + a * LH + h]))
    for c in local:
        c.start()

    key_block = lax.broadcasted_iota(jnp.int32, (NB, LEN), 1) // BLK
    entry = lax.broadcasted_iota(jnp.int32, (NB, 1), 0)
    lane = lax.broadcasted_iota(jnp.int32, (1, HEADS), 1)
    for h in range(LH):
        mine = lane == me * LH + h

        def mask_row(i, carry):
            count = jnp.sum(jnp.where(mine, kc_ref[pl.ds(i, 1), :], 0), axis=1, keepdims=True)
            listed = jnp.sum(jnp.where(mine, kb_ref[i], 0), axis=1, keepdims=True)
            listed = jnp.where(entry < count, listed, -1)
            hit = jnp.where(listed == key_block, 1.0, 0.0).astype(f32)
            found = jnp.max(hit, axis=0, keepdims=True)
            bias[h, i] = jnp.where(found > 0.5, 0.0, -jnp.inf).astype(f32)
            return carry

        lax.fori_loop(0, NB, mask_row, 0)

    pl.semaphore_wait(barrier, len(targets))

    up, down, across = (dp, seq_at(0, 1)), (dp, seq_at(0, 3)), (dp, seq_at(1, 0))

    def sem_of(dx, dy, part):
        return (order.index((dx % 2, dy % 4)) - 1) * 2 + part

    g_copies = {}

    def pass_on(dx, dy, part, way):
        dev, tdx, tdy = {"up": (up, dx, dy - 1), "down": (down, dx, dy + 1), "across": (across, dx + 1, dy)}[way]
        rows = pl.ds(part * HALF, HALF)
        n = sem_of(tdx, tdy, part)
        slot = slot_of[(dx % 2, dy % 4)]
        src = g_ref.at[rows] if (dx, dy) == (0, 0) else gall.at[slot, rows]
        c = remote(src, gall.at[slot, rows], g_send.at[n], g_recv.at[n], dev)
        c.start()
        g_copies[n] = c

    done = set()

    def arrived(dx, dy, part):
        n = sem_of(dx, dy, part)
        if n not in done:
            done.add(n)
            g_copies[n].wait_recv()

    for part in (0, 1):
        pass_on(0, 0, part, "across")
    pass_on(0, 0, 0, "up")
    pass_on(0, 0, 1, "down")
    pass_on(0, 0, 1, "up")
    pass_on(0, 0, 0, "down")

    w_copies = []
    for d in range(1, ZN):
        w_copies.append(remote(w_ref, wbuf.at[quad, z], w_send.at[d - 1], w_recv.at[d - 1], along_z[d - 1]))
    for c in w_copies:
        c.start()

    in_copies = []

    def send_inputs(h):
        for a, (src, dst) in enumerate(inputs):
            for i, p in enumerate(peers):
                n = (h * 3 + a) * 7 + i
                c = remote(src.at[:, cols(p, h)], dst.at[h, me], in_send.at[n], in_recv.at[n], (dp, p))
                c.start()
                in_copies.append(c)

    def turn(step):
        slot = slot_of[order[step]]
        place = pl.ds(pl.multiple_of(slot * ROWS, 128), ROWS)

        def piece(i, carry):
            cc = pl.ds(pl.multiple_of(i * CHUNK, 128), CHUNK)
            gturn[cc, place] = gall[slot, :, cc].T
            return carry

        lax.fori_loop(0, CW // CHUNK, piece, 0)

    def inputs_arrived(h):
        for c in in_copies[h * 21 : (h + 1) * 21]:
            c.wait_recv()

    def assemble(i, carry):
        group = jnp.concatenate([wbuf[q, i].astype(f32) for q in range(4)], axis=0)
        wt[pl.ds(pl.multiple_of(i * 4 * OWN, 32), 4 * OWN), :] = group.astype(bf)
        return carry

    far = (1 - xl) * 2 + core

    def head_gradients(column):
        first = column * 4
        part = dot_nn(gall[pl.ds(first, 4)].reshape(4 * ROWS, CW), wt[...]).astype(bf)
        rows = pl.ds(pl.multiple_of(first * ROWS, 4 * ROWS), 4 * ROWS)
        for h in range(LH):
            gheads[h, rows, :] = part[:, h * HD : (h + 1) * HD]

    scale = HD ** -0.5
    shards = TILE // ROWS

    def forward(h):
        key = kg[h].reshape(LEN, HD)

        def scores(i, carry):
            query = qg[h, pl.ds(i * shards, shards)].reshape(TILE, HD)
            work[pl.ds(pl.multiple_of(i * TILE, TILE), TILE), :] = dot_nt(query, key)
            return carry

        lax.fori_loop(0, LEN // TILE, scores, 0)

        def softmax(i, carry):
            mask = bias[h, i]
            for j in range(BLK // SUB):
                rows = pl.ds(pl.multiple_of(i * BLK + j * SUB, SUB), SUB)
                s = work[rows, :] * (scale * LOG2E) + mask
                expo = jnp.exp2(s - jnp.max(s, axis=-1, keepdims=True))
                inverse[h % 2, rows, :] = 1.0 / jnp.sum(expo, axis=-1, keepdims=True)
                expos[h % 2, rows, :] = expo
                half[rows, :] = expo.astype(bf)
            return carry

        lax.fori_loop(0, NB, softmax, 0)

        def mix(i, carry):
            rows = pl.ds(pl.multiple_of(i * TILE, TILE), TILE)
            part = dot_nn(half[rows, :], vg[h].reshape(LEN, HD)) * inverse[h % 2, rows, :]
            wide[h % 2, rows, :] = part
            outs[rows, h * HD : (h + 1) * HD] = part.astype(bf)
            return carry

        lax.fori_loop(0, LEN // TILE, mix, 0)

    def weight_gradient(first, count):
        group = CW // 4
        mine = slice(first * HD, (first + count) * HD)

        def product(i, carry):
            part = dot_nn(gturn[pl.ds(pl.multiple_of(i * group, 128), group), :], outs[:, mine])
            for n in range(count):
                one = part[:, n * HD : (n + 1) * HD].reshape(4, 4, OWN, HD).astype(bf)
                for q in range(4):
                    rsrc[first + n, q, pl.ds(i * 4, 4)] = one[:, q]
            return carry

        lax.fori_loop(0, 4, product, 0)

    pair, sides, zs = {}, {}, {}

    def sum_pair(h):
        pair[h] = [
            remote(
                rsrc.at[h, x * 2 + 1 - core], r1.at[h, x], r_send.at[h * 18 + x], r_recv.at[h * 18 + x], mate
            )
            for x in range(2)
        ]
        for c in pair[h]:
            c.start()

    def sum_side(h):
        for c in pair[h]:
            c.wait_recv()

        def add(i, carry):
            t1[h, i] = (rsrc[h, far, i].astype(f32) + r1[h, 1 - xl, i].astype(f32)).astype(bf)
            return carry

        lax.fori_loop(0, ZN, add, 0)
        sides[h] = remote(t1.at[h], r2.at[h], r_send.at[h * 18 + 2], r_recv.at[h * 18 + 2], side)
        sides[h].start()

    def sum_z(h):
        sides[h].wait_recv()

        def add(i, carry):
            t2[h, i] = (rsrc[h, quad, i].astype(f32) + r1[h, xl, i].astype(f32) + r2[h, i].astype(f32)).astype(bf)
            return carry

        lax.fori_loop(0, ZN, add, 0)
        zs[h] = []
        for d in range(1, ZN):
            n = h * 18 + 2 + d
            zs[h].append(
                remote(t2.at[h, (z + d) % ZN], r3.at[h, d - 1], r_send.at[n], r_recv.at[n], along_z[d - 1])
            )
        for c in zs[h]:
            c.start()

    def sum_last(h):
        total = t2[h, z].astype(f32)
        for d, c in enumerate(zs[h]):
            c.wait_recv()
            total = total + r3[h, d].astype(f32)
        dw_out[:, h * HD : (h + 1) * HD] = total

    o_copies = []

    def send_back(h, a, src, dst):
        c = pltpu.make_async_copy(src.at[h, me], dst.at[:, cols(me, h)], loc.at[11 + h * 2 + a])
        c.start()
        o_copies.append((True, c))
        for i, p in enumerate(peers):
            n = (h * 2 + a) * 7 + i
            c = remote(src.at[h, p], dst.at[:, cols(me, h)], o_send.at[n], o_recv.at[n], (dp, p))
            c.start()
            o_copies.append((False, c))

    def backward(h, between):
        key = kg[h].reshape(LEN, HD)
        value = vg[h].reshape(LEN, HD)

        def products(i, carry):
            rows = pl.ds(pl.multiple_of(i * TILE, TILE), TILE)
            work[rows, :] = dot_nt(gheads[h, rows, :], value)
            return carry

        lax.fori_loop(0, LEN // TILE, products, 0)

        def softmax_grad(i, carry):
            for j in range(BLK // SUB):
                rows = pl.ds(pl.multiple_of(i * BLK + j * SUB, SUB), SUB)
                delta = jnp.sum(wide[h % 2, rows, :] * gheads[h, rows, :].astype(f32), axis=-1, keepdims=True)
                factor = inverse[h % 2, rows, :] * scale
                half[rows, :] = (expos[h % 2, rows, :] * ((work[rows, :] - delta) * factor)).astype(bf)
            return carry

        lax.fori_loop(0, NB, softmax_grad, 0)
        between()

        def query_grad(i, carry):
            rows = pl.ds(pl.multiple_of(i * TILE, TILE), TILE)
            part = dot_nn(half[rows, :], key).astype(bf)
            dqb[h, pl.ds(i * shards, shards)] = part.reshape(shards, ROWS, HD)
            return carry

        lax.fori_loop(0, LEN // TILE, query_grad, 0)
        send_back(h, 0, dqb, dq_out)

        def key_grad(i, carry):
            rows = pl.ds(pl.multiple_of(i * TILE, TILE), TILE)
            part = dot_tn(half[:, rows], qg[h].reshape(LEN, HD)).astype(bf)
            dkb[h, pl.ds(i * shards, shards)] = part.reshape(shards, ROWS, HD)
            return carry

        lax.fori_loop(0, LEN // TILE, key_grad, 0)
        send_back(h, 1, dkb, dk_out)

    send_inputs(0)
    send_inputs(1)
    arrived(0, 3, 0)
    pass_on(0, 3, 0, "up")
    pass_on(0, 3, 0, "across")
    arrived(0, 1, 1)
    pass_on(0, 1, 1, "down")
    pass_on(0, 1, 1, "across")
    arrived(1, 0, 0)
    pass_on(1, 0, 0, "down")
    arrived(1, 0, 1)
    pass_on(1, 0, 1, "up")
    for c in local:
        c.wait()
    turn(0)
    inputs_arrived(0)
    forward(0)

    for c in w_copies:
        c.wait_recv()
    plane = [
        remote(wbuf.at[quad], wbuf.at[quad], w_send.at[15], w_recv.at[15], mate),
        remote(wbuf.at[quad], wbuf.at[quad], w_send.at[16], w_recv.at[16], side),
    ]
    for c in plane:
        c.start()
    inputs_arrived(1)
    forward(1)
    arrived(1, 3, 0)
    pass_on(1, 3, 0, "up")
    arrived(1, 1, 1)
    pass_on(1, 1, 1, "down")
    send_inputs(2)
    for step in range(1, 5):
        for part in (0, 1):
            arrived(*order[step], part)
        turn(step)
    plane[1].wait_recv()
    plane.append(remote(wbuf.at[far], wbuf.at[far], w_send.at[17], w_recv.at[17], mate))
    plane[2].start()
    plane[0].wait_recv()
    plane[2].wait_recv()
    lax.fori_loop(0, ZN, assemble, 0)
    head_gradients(xh)
    for step in range(5, SEQ):
        for part in (0, 1):
            arrived(*order[step], part)
        turn(step)
    weight_gradient(0, 2)
    sum_pair(0)
    sum_pair(1)
    head_gradients(1 - xh)
    backward(0, lambda: None)
    sum_side(0)
    sum_side(1)
    backward(1, lambda: None)
    inputs_arrived(2)
    forward(2)
    weight_gradient(2, 1)
    sum_pair(2)
    sum_z(0)
    sum_z(1)
    backward(2, lambda: sum_side(2))
    sum_last(0)
    sum_z(2)
    sum_last(1)
    sum_last(2)

    for here, c in o_copies:
        c.wait()
    for c in in_copies + w_copies + plane + list(g_copies.values()):
        c.wait_send()
    for h in range(LH):
        for c in pair[h] + [sides[h]] + zs[h]:
            c.wait_send()


def per_device(queries, key_states, value_states, grad_out, out_weight, key_blocks, key_count):
    bf, f32 = jnp.bfloat16, jnp.float32
    vmem = pl.BlockSpec(memory_space=pltpu.VMEM)
    dma = pltpu.SemaphoreType.DMA
    head_rows = pltpu.VMEM((LH, SEQ, ROWS, HD), bf)
    grad_q, grad_k, grad_w = pl.pallas_call(
        kernel,
        name="bigbird_backward",
        out_shape=(
            jax.ShapeDtypeStruct((ROWS, HEADS * HD), bf),
            jax.ShapeDtypeStruct((ROWS, HEADS * HD), bf),
            jax.ShapeDtypeStruct((OWN, LW), f32),
        ),
        in_specs=[vmem] * 7,
        out_specs=(vmem, vmem, vmem),
        scratch_shapes=[
            head_rows, head_rows, head_rows,
            pltpu.VMEM((SEQ, ROWS, CW), bf),
            pltpu.VMEM((CW, LEN), bf),
            pltpu.VMEM((4, ZN, OWN, LW), bf),
            pltpu.VMEM((CW, LW), bf),
            pltpu.VMEM((LH, NB, 1, LEN), f32),
            pltpu.VMEM((LEN, LEN), f32),
            pltpu.VMEM((2, LEN, LEN), f32),
            pltpu.VMEM((LEN, LEN), bf),
            pltpu.VMEM((LEN, LW), bf),
            pltpu.VMEM((2, LEN, HD), f32),
            pltpu.VMEM((2, LEN, 1), f32),
            pltpu.VMEM((LH, LEN, HD), bf),
            head_rows, head_rows,
            pltpu.VMEM((LH, 4, ZN, OWN, HD), bf),
            pltpu.VMEM((LH, 2, ZN, OWN, HD), bf),
            pltpu.VMEM((LH, ZN, OWN, HD), bf),
            pltpu.VMEM((LH, ZN, OWN, HD), bf),
            pltpu.VMEM((LH, ZN, OWN, HD), bf),
            pltpu.VMEM((LH, ZN - 1, OWN, HD), bf),
            dma((63,)), dma((63,)), dma((17,)),
            dma((14,)), dma((14,)),
            dma((18,)), dma((18,)),
            dma((42,)), dma((42,)),
            dma((54,)), dma((54,)),
        ],
        compiler_params=pltpu.CompilerParams(
            collective_id=0, has_side_effects=True, vmem_limit_bytes=60 * 1024 * 1024
        ),
    )(queries, key_states, value_states, grad_out, out_weight.T, key_blocks.transpose(1, 2, 0), key_count.T)
    return grad_q, grad_k, grad_w.T


def solution(mesh):
    return jax.shard_map(
        per_device,
        mesh=mesh,
        in_specs=(
            P(("dp", "seq"), None),
            P(("dp", "seq"), None),
            P(("dp", "seq"), None),
            P(("dp", "seq"), None),
            P("seq", "dp"),
            P(),
            P(),
        ),
        out_specs=(P(("dp", "seq"), None), P(("dp", "seq"), None), P("seq", "dp")),
        check_vma=False,
    )
```

```python
import jax
import jax.numpy as jnp
from jax import lax
from jax.experimental import pallas as pl
from jax.experimental.pallas import tpu as pltpu
from jax.sharding import PartitionSpec as P

HEADS = 24
HD = 128
BLK = 64
NB = 16
LOG2E = 1.4426950408889634
MESH = pl.DeviceIdType.MESH

SEQ = 8
ROWS = 128
LEN = SEQ * ROWS
LH = HEADS // SEQ
LW = LH * HD
CW = 2560
HALF = ROWS // 2
ZN = 16
OWN = CW // 64
TILE = 512
SUB = 16
CHUNK = 512


def dot_nn(a, b):
    return lax.dot_general(a, b, (((1,), (0,)), ((), ())), preferred_element_type=jnp.float32)


def dot_nt(a, b):
    return lax.dot_general(a, b, (((1,), (1,)), ((), ())), preferred_element_type=jnp.float32)


def dot_tn(a, b):
    return lax.dot_general(a, b, (((0,), (0,)), ((), ())), preferred_element_type=jnp.float32)


def remote(src, dst, ssem, rsem, dev):
    return pltpu.make_async_remote_copy(
        src_ref=src, dst_ref=dst, send_sem=ssem, recv_sem=rsem, device_id=dev, device_id_type=MESH
    )


def kernel(
    q_ref, k_ref, v_ref, g_ref, w_ref, kb_ref, kc_ref,
    dq_out, dk_out, dw_out,
    qg, kg, vg, gall, gturn, wbuf, wt, bias, work, expos, half, outs, wide, inverse, gheads, dqb, dkb,
    rsrc, r1, t1, r2, t2, r3,
    in_send, in_recv, loc, g_send, g_recv, w_send, w_recv, o_send, o_recv, r_send, r_recv,
):
    bf, f32 = jnp.bfloat16, jnp.float32
    dp = lax.axis_index("dp")
    me = lax.axis_index("seq")
    z = dp // 4
    quad = dp % 4
    xl = quad // 2
    core = quad % 2
    xh = me // 4
    y = me % 4

    def seq_at(dx, dy):
        return ((xh + dx) % 2) * 4 + (y + dy) % 4

    order = [(0, 0), (0, 3), (0, 1), (1, 0), (0, 2), (1, 3), (1, 1), (1, 2)]
    slot_of = {o: seq_at(*o) for o in order}
    peers = [slot_of[o] for o in order[1:]]
    mate = (z * 4 + xl * 2 + (1 - core), me)
    side = (z * 4 + (1 - xl) * 2 + core, me)
    along_z = [(((z + d) % ZN) * 4 + quad, me) for d in range(1, ZN)]

    barrier = pltpu.get_barrier_semaphore()
    targets = along_z + [(dp, p) for p in peers] + [mate, side]
    for t in targets:
        pl.semaphore_signal(barrier, inc=1, device_id=t, device_id_type=MESH)

    def cols(p, h):
        return pl.ds(pl.multiple_of(p * LW + h * HD, 128), HD)

    inputs = ((q_ref, qg), (k_ref, kg), (v_ref, vg))
    local = [pltpu.make_async_copy(g_ref, gall.at[me], loc.at[0])]
    local.append(pltpu.make_async_copy(w_ref, wbuf.at[quad, z], loc.at[1]))
    for a, (src, dst) in enumerate(inputs):
        for h in range(LH):
            local.append(pltpu.make_async_copy(src.at[:, cols(me, h)], dst.at[h, me], loc.at[2 + a * LH + h]))
    for c in local:
        c.start()

    key_block = lax.broadcasted_iota(jnp.int32, (NB, LEN), 1) // BLK
    entry = lax.broadcasted_iota(jnp.int32, (NB, 1), 0)
    lane = lax.broadcasted_iota(jnp.int32, (1, HEADS), 1)
    for h in range(LH):
        mine = lane == me * LH + h

        def mask_row(i, carry):
            count = jnp.sum(jnp.where(mine, kc_ref[pl.ds(i, 1), :], 0), axis=1, keepdims=True)
            listed = jnp.sum(jnp.where(mine, kb_ref[i], 0), axis=1, keepdims=True)
            listed = jnp.where(entry < count, listed, -1)
            hit = jnp.where(listed == key_block, 1.0, 0.0).astype(f32)
            found = jnp.max(hit, axis=0, keepdims=True)
            bias[h, i] = jnp.where(found > 0.5, 0.0, -jnp.inf).astype(f32)
            return carry

        lax.fori_loop(0, NB, mask_row, 0)

    pl.semaphore_wait(barrier, len(targets))

    up, down, across = (dp, seq_at(0, 1)), (dp, seq_at(0, 3)), (dp, seq_at(1, 0))

    def sem_of(dx, dy, part):
        return (order.index((dx % 2, dy % 4)) - 1) * 2 + part

    g_copies = {}

    def pass_on(dx, dy, part, way):
        dev, tdx, tdy = {"up": (up, dx, dy - 1), "down": (down, dx, dy + 1), "across": (across, dx + 1, dy)}[way]
        rows = pl.ds(part * HALF, HALF)
        n = sem_of(tdx, tdy, part)
        slot = slot_of[(dx % 2, dy % 4)]
        src = g_ref.at[rows] if (dx, dy) == (0, 0) else gall.at[slot, rows]
        c = remote(src, gall.at[slot, rows], g_send.at[n], g_recv.at[n], dev)
        c.start()
        g_copies[n] = c

    done = set()

    def arrived(dx, dy, part):
        n = sem_of(dx, dy, part)
        if n not in done:
            done.add(n)
            g_copies[n].wait_recv()

    for part in (0, 1):
        pass_on(0, 0, part, "across")
    pass_on(0, 0, 0, "up")
    pass_on(0, 0, 1, "down")
    pass_on(0, 0, 1, "up")
    pass_on(0, 0, 0, "down")

    w_copies = []
    for d in range(1, ZN):
        w_copies.append(remote(w_ref, wbuf.at[quad, z], w_send.at[d - 1], w_recv.at[d - 1], along_z[d - 1]))
    for c in w_copies:
        c.start()

    in_copies = []

    def send_inputs(h):
        for a, (src, dst) in enumerate(inputs):
            for i, p in enumerate(peers):
                n = (h * 3 + a) * 7 + i
                c = remote(src.at[:, cols(p, h)], dst.at[h, me], in_send.at[n], in_recv.at[n], (dp, p))
                c.start()
                in_copies.append(c)

    def turn(step):
        slot = slot_of[order[step]]
        place = pl.ds(pl.multiple_of(slot * ROWS, 128), ROWS)

        def piece(i, carry):
            cc = pl.ds(pl.multiple_of(i * CHUNK, 128), CHUNK)
            gturn[cc, place] = gall[slot, :, cc].T
            return carry

        lax.fori_loop(0, CW // CHUNK, piece, 0)

    def inputs_arrived(h):
        for c in in_copies[h * 21 : (h + 1) * 21]:
            c.wait_recv()

    def assemble(i, carry):
        group = jnp.concatenate([wbuf[q, i].astype(f32) for q in range(4)], axis=0)
        wt[pl.ds(pl.multiple_of(i * 4 * OWN, 32), 4 * OWN), :] = group.astype(bf)
        return carry

    far = (1 - xl) * 2 + core

    def head_gradients(column):
        first = column * 4
        part = dot_nn(gall[pl.ds(first, 4)].reshape(4 * ROWS, CW), wt[...]).astype(bf)
        rows = pl.ds(pl.multiple_of(first * ROWS, 4 * ROWS), 4 * ROWS)
        for h in range(LH):
            gheads[h, rows, :] = part[:, h * HD : (h + 1) * HD]

    scale = HD ** -0.5
    shards = TILE // ROWS

    def forward(h):
        key = kg[h].reshape(LEN, HD)

        def scores(i, carry):
            query = qg[h, pl.ds(i * shards, shards)].reshape(TILE, HD)
            work[pl.ds(pl.multiple_of(i * TILE, TILE), TILE), :] = dot_nt(query, key)
            return carry

        lax.fori_loop(0, LEN // TILE, scores, 0)

        def softmax(i, carry):
            mask = bias[h, i]
            for j in range(BLK // SUB):
                rows = pl.ds(pl.multiple_of(i * BLK + j * SUB, SUB), SUB)
                s = work[rows, :] * (scale * LOG2E) + mask
                expo = jnp.exp2(s - jnp.max(s, axis=-1, keepdims=True))
                inverse[h % 2, rows, :] = 1.0 / jnp.sum(expo, axis=-1, keepdims=True)
                expos[h % 2, rows, :] = expo
                half[rows, :] = expo.astype(bf)
            return carry

        lax.fori_loop(0, NB, softmax, 0)

        def mix(i, carry):
            rows = pl.ds(pl.multiple_of(i * TILE, TILE), TILE)
            part = dot_nn(half[rows, :], vg[h].reshape(LEN, HD)) * inverse[h % 2, rows, :]
            wide[h % 2, rows, :] = part
            outs[rows, h * HD : (h + 1) * HD] = part.astype(bf)
            return carry

        lax.fori_loop(0, LEN // TILE, mix, 0)

    def weight_gradient(first, count):
        group = CW // 4
        mine = slice(first * HD, (first + count) * HD)

        def product(i, carry):
            part = dot_nn(gturn[pl.ds(pl.multiple_of(i * group, 128), group), :], outs[:, mine])
            for n in range(count):
                one = part[:, n * HD : (n + 1) * HD].reshape(4, 4, OWN, HD).astype(bf)
                for q in range(4):
                    rsrc[first + n, q, pl.ds(i * 4, 4)] = one[:, q]
            return carry

        lax.fori_loop(0, 4, product, 0)

    pair, sides, zs = {}, {}, {}

    def sum_pair(h):
        pair[h] = [
            remote(
                rsrc.at[h, x * 2 + 1 - core], r1.at[h, x], r_send.at[h * 18 + x], r_recv.at[h * 18 + x], mate
            )
            for x in range(2)
        ]
        for c in pair[h]:
            c.start()

    def sum_side(h):
        for c in pair[h]:
            c.wait_recv()

        def add(i, carry):
            t1[h, i] = (rsrc[h, far, i].astype(f32) + r1[h, 1 - xl, i].astype(f32)).astype(bf)
            return carry

        lax.fori_loop(0, ZN, add, 0)
        sides[h] = remote(t1.at[h], r2.at[h], r_send.at[h * 18 + 2], r_recv.at[h * 18 + 2], side)
        sides[h].start()

    def sum_z(h):
        sides[h].wait_recv()

        def add(i, carry):
            t2[h, i] = (rsrc[h, quad, i].astype(f32) + r1[h, xl, i].astype(f32) + r2[h, i].astype(f32)).astype(bf)
            return carry

        lax.fori_loop(0, ZN, add, 0)
        zs[h] = []
        for d in range(1, ZN):
            n = h * 18 + 2 + d
            zs[h].append(
                remote(t2.at[h, (z + d) % ZN], r3.at[h, d - 1], r_send.at[n], r_recv.at[n], along_z[d - 1])
            )
        for c in zs[h]:
            c.start()

    def sum_last(h):
        total = t2[h, z].astype(f32)
        for d, c in enumerate(zs[h]):
            c.wait_recv()
            total = total + r3[h, d].astype(f32)
        dw_out[:, h * HD : (h + 1) * HD] = total

    o_copies = []

    def send_back(h, a, src, dst):
        c = pltpu.make_async_copy(src.at[h, me], dst.at[:, cols(me, h)], loc.at[11 + h * 2 + a])
        c.start()
        o_copies.append((True, c))
        for i, p in enumerate(peers):
            n = (h * 2 + a) * 7 + i
            c = remote(src.at[h, p], dst.at[:, cols(me, h)], o_send.at[n], o_recv.at[n], (dp, p))
            c.start()
            o_copies.append((False, c))

    def backward(h, between):
        key = kg[h].reshape(LEN, HD)
        value = vg[h].reshape(LEN, HD)

        def products(i, carry):
            rows = pl.ds(pl.multiple_of(i * TILE, TILE), TILE)
            work[rows, :] = dot_nt(gheads[h, rows, :], value)
            return carry

        lax.fori_loop(0, LEN // TILE, products, 0)

        def softmax_grad(i, carry):
            for j in range(BLK // SUB):
                rows = pl.ds(pl.multiple_of(i * BLK + j * SUB, SUB), SUB)
                delta = jnp.sum(wide[h % 2, rows, :] * gheads[h, rows, :].astype(f32), axis=-1, keepdims=True)
                factor = inverse[h % 2, rows, :] * scale
                half[rows, :] = (expos[h % 2, rows, :] * ((work[rows, :] - delta) * factor)).astype(bf)
            return carry

        lax.fori_loop(0, NB, softmax_grad, 0)
        between()

        def query_grad(i, carry):
            rows = pl.ds(pl.multiple_of(i * TILE, TILE), TILE)
            part = dot_nn(half[rows, :], key).astype(bf)
            dqb[h, pl.ds(i * shards, shards)] = part.reshape(shards, ROWS, HD)
            return carry

        lax.fori_loop(0, LEN // TILE, query_grad, 0)
        send_back(h, 0, dqb, dq_out)

        def key_grad(i, carry):
            rows = pl.ds(pl.multiple_of(i * TILE, TILE), TILE)
            part = dot_tn(half[:, rows], qg[h].reshape(LEN, HD)).astype(bf)
            dkb[h, pl.ds(i * shards, shards)] = part.reshape(shards, ROWS, HD)
            return carry

        lax.fori_loop(0, LEN // TILE, key_grad, 0)
        send_back(h, 1, dkb, dk_out)

    send_inputs(0)
    send_inputs(1)
    arrived(0, 3, 0)
    pass_on(0, 3, 0, "up")
    pass_on(0, 3, 0, "across")
    arrived(0, 1, 1)
    pass_on(0, 1, 1, "down")
    pass_on(0, 1, 1, "across")
    arrived(1, 0, 0)
    pass_on(1, 0, 0, "down")
    arrived(1, 0, 1)
    pass_on(1, 0, 1, "up")
    for c in local:
        c.wait()
    turn(0)
    inputs_arrived(0)
    forward(0)

    for c in w_copies:
        c.wait_recv()
    plane = [
        remote(wbuf.at[quad], wbuf.at[quad], w_send.at[15], w_recv.at[15], mate),
        remote(wbuf.at[quad], wbuf.at[quad], w_send.at[16], w_recv.at[16], side),
    ]
    for c in plane:
        c.start()
    inputs_arrived(1)
    forward(1)
    arrived(1, 3, 0)
    pass_on(1, 3, 0, "up")
    arrived(1, 1, 1)
    pass_on(1, 1, 1, "down")
    send_inputs(2)
    for step in range(1, 5):
        for part in (0, 1):
            arrived(*order[step], part)
        turn(step)
    plane[1].wait_recv()
    plane.append(remote(wbuf.at[far], wbuf.at[far], w_send.at[17], w_recv.at[17], mate))
    plane[2].start()
    plane[0].wait_recv()
    plane[2].wait_recv()
    lax.fori_loop(0, ZN, assemble, 0)
    head_gradients(xh)
    for step in range(5, SEQ):
        for part in (0, 1):
            arrived(*order[step], part)
        turn(step)
    weight_gradient(0, 2)
    sum_pair(0)
    sum_pair(1)
    head_gradients(1 - xh)
    backward(0, lambda: None)
    sum_side(0)
    sum_side(1)
    inputs_arrived(2)
    forward(2)
    weight_gradient(2, 1)
    sum_pair(2)
    sum_z(0)
    sum_z(1)
    backward(1, lambda: sum_side(2))
    backward(2, lambda: sum_z(2))
    sum_last(0)
    sum_last(1)
    sum_last(2)

    for here, c in o_copies:
        c.wait()
    for c in in_copies + w_copies + plane + list(g_copies.values()):
        c.wait_send()
    for h in range(LH):
        for c in pair[h] + [sides[h]] + zs[h]:
            c.wait_send()


def per_device(queries, key_states, value_states, grad_out, out_weight, key_blocks, key_count):
    bf, f32 = jnp.bfloat16, jnp.float32
    vmem = pl.BlockSpec(memory_space=pltpu.VMEM)
    dma = pltpu.SemaphoreType.DMA
    head_rows = pltpu.VMEM((LH, SEQ, ROWS, HD), bf)
    grad_q, grad_k, grad_w = pl.pallas_call(
        kernel,
        name="bigbird_backward",
        out_shape=(
            jax.ShapeDtypeStruct((ROWS, HEADS * HD), bf),
            jax.ShapeDtypeStruct((ROWS, HEADS * HD), bf),
            jax.ShapeDtypeStruct((OWN, LW), f32),
        ),
        in_specs=[vmem] * 7,
        out_specs=(vmem, vmem, vmem),
        scratch_shapes=[
            head_rows, head_rows, head_rows,
            pltpu.VMEM((SEQ, ROWS, CW), bf),
            pltpu.VMEM((CW, LEN), bf),
            pltpu.VMEM((4, ZN, OWN, LW), bf),
            pltpu.VMEM((CW, LW), bf),
            pltpu.VMEM((LH, NB, 1, LEN), f32),
            pltpu.VMEM((LEN, LEN), f32),
            pltpu.VMEM((2, LEN, LEN), f32),
            pltpu.VMEM((LEN, LEN), bf),
            pltpu.VMEM((LEN, LW), bf),
            pltpu.VMEM((2, LEN, HD), f32),
            pltpu.VMEM((2, LEN, 1), f32),
            pltpu.VMEM((LH, LEN, HD), bf),
            head_rows, head_rows,
            pltpu.VMEM((LH, 4, ZN, OWN, HD), bf),
            pltpu.VMEM((LH, 2, ZN, OWN, HD), bf),
            pltpu.VMEM((LH, ZN, OWN, HD), bf),
            pltpu.VMEM((LH, ZN, OWN, HD), bf),
            pltpu.VMEM((LH, ZN, OWN, HD), bf),
            pltpu.VMEM((LH, ZN - 1, OWN, HD), bf),
            dma((63,)), dma((63,)), dma((17,)),
            dma((14,)), dma((14,)),
            dma((18,)), dma((18,)),
            dma((42,)), dma((42,)),
            dma((54,)), dma((54,)),
        ],
        compiler_params=pltpu.CompilerParams(
            collective_id=0, has_side_effects=True, vmem_limit_bytes=60 * 1024 * 1024
        ),
    )(queries, key_states, value_states, grad_out, out_weight.T, key_blocks.transpose(1, 2, 0), key_count.T)
    return grad_q, grad_k, grad_w.T


def solution(mesh):
    return jax.shard_map(
        per_device,
        mesh=mesh,
        in_specs=(
            P(("dp", "seq"), None),
            P(("dp", "seq"), None),
            P(("dp", "seq"), None),
            P(("dp", "seq"), None),
            P("seq", "dp"),
            P(),
            P(),
        ),
        out_specs=(P(("dp", "seq"), None), P(("dp", "seq"), None), P("seq", "dp")),
        check_vma=False,
    )
```

```python
import jax
import jax.numpy as jnp
from jax import lax
from jax.experimental import pallas as pl
from jax.experimental.pallas import tpu as pltpu
from jax.sharding import PartitionSpec as P

HEADS = 24
HD = 128
BLK = 64
NB = 16
LOG2E = 1.4426950408889634
MESH = pl.DeviceIdType.MESH

SEQ = 8
ROWS = 128
LEN = SEQ * ROWS
LH = HEADS // SEQ
LW = LH * HD
CW = 2560
HALF = ROWS // 2
ZN = 16
OWN = CW // 64
TILE = 512
SUB = 16
CHUNK = 512


def dot_nn(a, b):
    return lax.dot_general(a, b, (((1,), (0,)), ((), ())), preferred_element_type=jnp.float32)


def dot_nt(a, b):
    return lax.dot_general(a, b, (((1,), (1,)), ((), ())), preferred_element_type=jnp.float32)


def dot_tn(a, b):
    return lax.dot_general(a, b, (((0,), (0,)), ((), ())), preferred_element_type=jnp.float32)


def remote(src, dst, ssem, rsem, dev):
    return pltpu.make_async_remote_copy(
        src_ref=src, dst_ref=dst, send_sem=ssem, recv_sem=rsem, device_id=dev, device_id_type=MESH
    )


def kernel(
    q_ref, k_ref, v_ref, g_ref, w_ref, kb_ref, kc_ref,
    dq_out, dk_out, dw_out,
    qg, kg, vg, gall, gturn, wbuf, wt, bias, work, expos, half, outs, wide, inverse, gheads, dqb, dkb,
    rsrc, r1, t1, r2, t2, r3,
    in_send, in_recv, loc, g_send, g_recv, w_send, w_recv, o_send, o_recv, r_send, r_recv,
):
    bf, f32 = jnp.bfloat16, jnp.float32
    dp = lax.axis_index("dp")
    me = lax.axis_index("seq")
    z = dp // 4
    quad = dp % 4
    xl = quad // 2
    core = quad % 2
    xh = me // 4
    y = me % 4

    def seq_at(dx, dy):
        return ((xh + dx) % 2) * 4 + (y + dy) % 4

    order = [(0, 0), (0, 3), (0, 1), (1, 0), (0, 2), (1, 3), (1, 1), (1, 2)]
    slot_of = {o: seq_at(*o) for o in order}
    peers = [slot_of[o] for o in order[1:]]
    mate = (z * 4 + xl * 2 + (1 - core), me)
    side = (z * 4 + (1 - xl) * 2 + core, me)
    along_z = [(((z + d) % ZN) * 4 + quad, me) for d in range(1, ZN)]

    barrier = pltpu.get_barrier_semaphore()
    targets = along_z + [(dp, p) for p in peers] + [mate, side]
    for t in targets:
        pl.semaphore_signal(barrier, inc=1, device_id=t, device_id_type=MESH)

    def cols(p, h):
        return pl.ds(pl.multiple_of(p * LW + h * HD, 128), HD)

    inputs = ((q_ref, qg), (k_ref, kg), (v_ref, vg))
    local = [pltpu.make_async_copy(g_ref, gall.at[me], loc.at[0])]
    local.append(pltpu.make_async_copy(w_ref, wbuf.at[quad, z], loc.at[1]))
    for a, (src, dst) in enumerate(inputs):
        for h in range(LH):
            local.append(pltpu.make_async_copy(src.at[:, cols(me, h)], dst.at[h, me], loc.at[2 + a * LH + h]))
    for c in local:
        c.start()

    key_block = lax.broadcasted_iota(jnp.int32, (NB, LEN), 1) // BLK
    entry = lax.broadcasted_iota(jnp.int32, (NB, 1), 0)
    lane = lax.broadcasted_iota(jnp.int32, (1, HEADS), 1)
    for h in range(LH):
        mine = lane == me * LH + h

        def mask_row(i, carry):
            count = jnp.sum(jnp.where(mine, kc_ref[pl.ds(i, 1), :], 0), axis=1, keepdims=True)
            listed = jnp.sum(jnp.where(mine, kb_ref[i], 0), axis=1, keepdims=True)
            listed = jnp.where(entry < count, listed, -1)
            hit = jnp.where(listed == key_block, 1.0, 0.0).astype(f32)
            found = jnp.max(hit, axis=0, keepdims=True)
            bias[h, i] = jnp.where(found > 0.5, 0.0, -jnp.inf).astype(f32)
            return carry

        lax.fori_loop(0, NB, mask_row, 0)

    pl.semaphore_wait(barrier, len(targets))

    up, down, across = (dp, seq_at(0, 1)), (dp, seq_at(0, 3)), (dp, seq_at(1, 0))

    def sem_of(dx, dy, part):
        return (order.index((dx % 2, dy % 4)) - 1) * 2 + part

    g_copies = {}

    def pass_on(dx, dy, part, way):
        dev, tdx, tdy = {"up": (up, dx, dy - 1), "down": (down, dx, dy + 1), "across": (across, dx + 1, dy)}[way]
        rows = pl.ds(part * HALF, HALF)
        n = sem_of(tdx, tdy, part)
        slot = slot_of[(dx % 2, dy % 4)]
        src = g_ref.at[rows] if (dx, dy) == (0, 0) else gall.at[slot, rows]
        c = remote(src, gall.at[slot, rows], g_send.at[n], g_recv.at[n], dev)
        c.start()
        g_copies[n] = c

    done = set()

    def arrived(dx, dy, part):
        n = sem_of(dx, dy, part)
        if n not in done:
            done.add(n)
            g_copies[n].wait_recv()

    for part in (0, 1):
        pass_on(0, 0, part, "across")
    pass_on(0, 0, 0, "up")
    pass_on(0, 0, 1, "down")
    pass_on(0, 0, 1, "up")
    pass_on(0, 0, 0, "down")

    w_copies = []
    for d in range(1, ZN):
        w_copies.append(remote(w_ref, wbuf.at[quad, z], w_send.at[d - 1], w_recv.at[d - 1], along_z[d - 1]))
    for c in w_copies:
        c.start()

    in_copies = []

    def send_inputs(h):
        for a, (src, dst) in enumerate(inputs):
            for i, p in enumerate(peers):
                n = (h * 3 + a) * 7 + i
                c = remote(src.at[:, cols(p, h)], dst.at[h, me], in_send.at[n], in_recv.at[n], (dp, p))
                c.start()
                in_copies.append(c)

    def turn(step):
        slot = slot_of[order[step]]
        place = pl.ds(pl.multiple_of(slot * ROWS, 128), ROWS)

        def piece(i, carry):
            cc = pl.ds(pl.multiple_of(i * CHUNK, 128), CHUNK)
            gturn[cc, place] = gall[slot, :, cc].T
            return carry

        lax.fori_loop(0, CW // CHUNK, piece, 0)

    def inputs_arrived(h):
        for c in in_copies[h * 21 : (h + 1) * 21]:
            c.wait_recv()

    def assemble(i, carry):
        group = jnp.concatenate([wbuf[q, i].astype(f32) for q in range(4)], axis=0)
        wt[pl.ds(pl.multiple_of(i * 4 * OWN, 32), 4 * OWN), :] = group.astype(bf)
        return carry

    far = (1 - xl) * 2 + core

    def head_gradients(column):
        first = column * 4
        part = dot_nn(gall[pl.ds(first, 4)].reshape(4 * ROWS, CW), wt[...]).astype(bf)
        rows = pl.ds(pl.multiple_of(first * ROWS, 4 * ROWS), 4 * ROWS)
        for h in range(LH):
            gheads[h, rows, :] = part[:, h * HD : (h + 1) * HD]

    scale = HD ** -0.5
    shards = TILE // ROWS

    def forward(h):
        key = kg[h].reshape(LEN, HD)

        def scores(i, carry):
            query = qg[h, pl.ds(i * shards, shards)].reshape(TILE, HD)
            work[pl.ds(pl.multiple_of(i * TILE, TILE), TILE), :] = dot_nt(query, key)
            return carry

        lax.fori_loop(0, LEN // TILE, scores, 0)

        def softmax(i, carry):
            mask = bias[h, i]
            for j in range(BLK // SUB):
                rows = pl.ds(pl.multiple_of(i * BLK + j * SUB, SUB), SUB)
                s = work[rows, :] * (scale * LOG2E) + mask
                expo = jnp.exp2(s - jnp.max(s, axis=-1, keepdims=True))
                inverse[h % 2, rows, :] = 1.0 / jnp.sum(expo, axis=-1, keepdims=True)
                expos[h % 2, rows, :] = expo
                half[rows, :] = expo.astype(bf)
            return carry

        lax.fori_loop(0, NB, softmax, 0)

        def mix(i, carry):
            rows = pl.ds(pl.multiple_of(i * TILE, TILE), TILE)
            part = dot_nn(half[rows, :], vg[h].reshape(LEN, HD)) * inverse[h % 2, rows, :]
            wide[h % 2, rows, :] = part
            outs[rows, h * HD : (h + 1) * HD] = part.astype(bf)
            return carry

        lax.fori_loop(0, LEN // TILE, mix, 0)

    def weight_gradient(first, count):
        group = CW // 4
        mine = slice(first * HD, (first + count) * HD)

        def product(i, carry):
            part = dot_nn(gturn[pl.ds(pl.multiple_of(i * group, 128), group), :], outs[:, mine])
            for n in range(count):
                one = part[:, n * HD : (n + 1) * HD].reshape(4, 4, OWN, HD).astype(bf)
                for q in range(4):
                    rsrc[first + n, q, pl.ds(i * 4, 4)] = one[:, q]
            return carry

        lax.fori_loop(0, 4, product, 0)

    pair, sides, zs = {}, {}, {}

    def sum_pair(h):
        pair[h] = [
            remote(
                rsrc.at[h, x * 2 + 1 - core], r1.at[h, x], r_send.at[h * 18 + x], r_recv.at[h * 18 + x], mate
            )
            for x in range(2)
        ]
        for c in pair[h]:
            c.start()

    def sum_side(h):
        for c in pair[h]:
            c.wait_recv()

        def add(i, carry):
            t1[h, i] = (rsrc[h, far, i].astype(f32) + r1[h, 1 - xl, i].astype(f32)).astype(bf)
            return carry

        lax.fori_loop(0, ZN, add, 0)
        sides[h] = remote(t1.at[h], r2.at[h], r_send.at[h * 18 + 2], r_recv.at[h * 18 + 2], side)
        sides[h].start()

    def sum_z(h):
        sides[h].wait_recv()

        def add(i, carry):
            t2[h, i] = (rsrc[h, quad, i].astype(f32) + r1[h, xl, i].astype(f32) + r2[h, i].astype(f32)).astype(bf)
            return carry

        lax.fori_loop(0, ZN, add, 0)
        zs[h] = []
        for d in range(1, ZN):
            n = h * 18 + 2 + d
            zs[h].append(
                remote(t2.at[h, (z + d) % ZN], r3.at[h, d - 1], r_send.at[n], r_recv.at[n], along_z[d - 1])
            )
        for c in zs[h]:
            c.start()

    def sum_last(h):
        total = t2[h, z].astype(f32)
        for d, c in enumerate(zs[h]):
            c.wait_recv()
            total = total + r3[h, d].astype(f32)
        dw_out[:, h * HD : (h + 1) * HD] = total

    o_copies = []

    def send_back(h, a, src, dst):
        c = pltpu.make_async_copy(src.at[h, me], dst.at[:, cols(me, h)], loc.at[11 + h * 2 + a])
        c.start()
        o_copies.append((True, c))
        for i, p in enumerate(peers):
            n = (h * 2 + a) * 7 + i
            c = remote(src.at[h, p], dst.at[:, cols(me, h)], o_send.at[n], o_recv.at[n], (dp, p))
            c.start()
            o_copies.append((False, c))

    def backward(h, between):
        key = kg[h].reshape(LEN, HD)
        value = vg[h].reshape(LEN, HD)

        def products(i, carry):
            rows = pl.ds(pl.multiple_of(i * TILE, TILE), TILE)
            work[rows, :] = dot_nt(gheads[h, rows, :], value)
            return carry

        lax.fori_loop(0, LEN // TILE, products, 0)

        def softmax_grad(i, carry):
            for j in range(BLK // SUB):
                rows = pl.ds(pl.multiple_of(i * BLK + j * SUB, SUB), SUB)
                delta = jnp.sum(wide[h % 2, rows, :] * gheads[h, rows, :].astype(f32), axis=-1, keepdims=True)
                factor = inverse[h % 2, rows, :] * scale
                half[rows, :] = (expos[h % 2, rows, :] * ((work[rows, :] - delta) * factor)).astype(bf)
            return carry

        lax.fori_loop(0, NB, softmax_grad, 0)
        between()

        def query_grad(i, carry):
            rows = pl.ds(pl.multiple_of(i * TILE, TILE), TILE)
            part = dot_nn(half[rows, :], key).astype(bf)
            dqb[h, pl.ds(i * shards, shards)] = part.reshape(shards, ROWS, HD)
            return carry

        lax.fori_loop(0, LEN // TILE, query_grad, 0)
        send_back(h, 0, dqb, dq_out)

        def key_grad(i, carry):
            rows = pl.ds(pl.multiple_of(i * TILE, TILE), TILE)
            part = dot_tn(half[:, rows], qg[h].reshape(LEN, HD)).astype(bf)
            dkb[h, pl.ds(i * shards, shards)] = part.reshape(shards, ROWS, HD)
            return carry

        lax.fori_loop(0, LEN // TILE, key_grad, 0)
        send_back(h, 1, dkb, dk_out)

    send_inputs(0)
    send_inputs(1)
    arrived(0, 3, 0)
    pass_on(0, 3, 0, "up")
    pass_on(0, 3, 0, "across")
    arrived(0, 1, 1)
    pass_on(0, 1, 1, "down")
    pass_on(0, 1, 1, "across")
    arrived(1, 0, 0)
    pass_on(1, 0, 0, "down")
    arrived(1, 0, 1)
    pass_on(1, 0, 1, "up")
    for c in local:
        c.wait()
    turn(0)
    inputs_arrived(0)
    forward(0)

    for c in w_copies:
        c.wait_recv()
    plane = [
        remote(wbuf.at[quad], wbuf.at[quad], w_send.at[15], w_recv.at[15], mate),
        remote(wbuf.at[quad], wbuf.at[quad], w_send.at[16], w_recv.at[16], side),
    ]
    for c in plane:
        c.start()
    inputs_arrived(1)
    forward(1)
    arrived(1, 3, 0)
    pass_on(1, 3, 0, "up")
    arrived(1, 1, 1)
    pass_on(1, 1, 1, "down")
    send_inputs(2)
    for step in range(1, 5):
        for part in (0, 1):
            arrived(*order[step], part)
        turn(step)
    plane[1].wait_recv()
    plane.append(remote(wbuf.at[far], wbuf.at[far], w_send.at[17], w_recv.at[17], mate))
    plane[2].start()
    plane[0].wait_recv()
    plane[2].wait_recv()
    lax.fori_loop(0, ZN, assemble, 0)
    head_gradients(xh)
    for step in range(5, SEQ):
        for part in (0, 1):
            arrived(*order[step], part)
        turn(step)
    weight_gradient(0, 2)
    sum_pair(0)
    sum_pair(1)
    head_gradients(1 - xh)
    sum_side(0)
    sum_side(1)
    backward(0, lambda: None)
    inputs_arrived(2)
    sum_z(0)
    forward(2)
    sum_z(1)
    weight_gradient(2, 1)
    sum_pair(2)
    backward(1, lambda: sum_side(2))
    backward(2, lambda: sum_z(2))
    sum_last(0)
    sum_last(1)
    sum_last(2)

    for here, c in o_copies:
        c.wait()
    for c in in_copies + w_copies + plane + list(g_copies.values()):
        c.wait_send()
    for h in range(LH):
        for c in pair[h] + [sides[h]] + zs[h]:
            c.wait_send()


def per_device(queries, key_states, value_states, grad_out, out_weight, key_blocks, key_count):
    bf, f32 = jnp.bfloat16, jnp.float32
    vmem = pl.BlockSpec(memory_space=pltpu.VMEM)
    dma = pltpu.SemaphoreType.DMA
    head_rows = pltpu.VMEM((LH, SEQ, ROWS, HD), bf)
    grad_q, grad_k, grad_w = pl.pallas_call(
        kernel,
        name="bigbird_backward",
        out_shape=(
            jax.ShapeDtypeStruct((ROWS, HEADS * HD), bf),
            jax.ShapeDtypeStruct((ROWS, HEADS * HD), bf),
            jax.ShapeDtypeStruct((OWN, LW), f32),
        ),
        in_specs=[vmem] * 7,
        out_specs=(vmem, vmem, vmem),
        scratch_shapes=[
            head_rows, head_rows, head_rows,
            pltpu.VMEM((SEQ, ROWS, CW), bf),
            pltpu.VMEM((CW, LEN), bf),
            pltpu.VMEM((4, ZN, OWN, LW), bf),
            pltpu.VMEM((CW, LW), bf),
            pltpu.VMEM((LH, NB, 1, LEN), f32),
            pltpu.VMEM((LEN, LEN), f32),
            pltpu.VMEM((2, LEN, LEN), f32),
            pltpu.VMEM((LEN, LEN), bf),
            pltpu.VMEM((LEN, LW), bf),
            pltpu.VMEM((2, LEN, HD), f32),
            pltpu.VMEM((2, LEN, 1), f32),
            pltpu.VMEM((LH, LEN, HD), bf),
            head_rows, head_rows,
            pltpu.VMEM((LH, 4, ZN, OWN, HD), bf),
            pltpu.VMEM((LH, 2, ZN, OWN, HD), bf),
            pltpu.VMEM((LH, ZN, OWN, HD), bf),
            pltpu.VMEM((LH, ZN, OWN, HD), bf),
            pltpu.VMEM((LH, ZN, OWN, HD), bf),
            pltpu.VMEM((LH, ZN - 1, OWN, HD), bf),
            dma((63,)), dma((63,)), dma((17,)),
            dma((14,)), dma((14,)),
            dma((18,)), dma((18,)),
            dma((42,)), dma((42,)),
            dma((54,)), dma((54,)),
        ],
        compiler_params=pltpu.CompilerParams(
            collective_id=0, has_side_effects=True, vmem_limit_bytes=60 * 1024 * 1024
        ),
    )(queries, key_states, value_states, grad_out, out_weight.T, key_blocks.transpose(1, 2, 0), key_count.T)
    return grad_q, grad_k, grad_w.T


def solution(mesh):
    return jax.shard_map(
        per_device,
        mesh=mesh,
        in_specs=(
            P(("dp", "seq"), None),
            P(("dp", "seq"), None),
            P(("dp", "seq"), None),
            P(("dp", "seq"), None),
            P("seq", "dp"),
            P(),
            P(),
        ),
        out_specs=(P(("dp", "seq"), None), P(("dp", "seq"), None), P("seq", "dp")),
        check_vma=False,
    )
```

```python
import jax
import jax.numpy as jnp
from jax import lax
from jax.experimental import pallas as pl
from jax.experimental.pallas import tpu as pltpu
from jax.sharding import PartitionSpec as P

HEADS = 24
HD = 128
BLK = 64
NB = 16
LOG2E = 1.4426950408889634
MESH = pl.DeviceIdType.MESH

SEQ = 8
ROWS = 128
LEN = SEQ * ROWS
LH = HEADS // SEQ
LW = LH * HD
CW = 2560
HALF = ROWS // 2
ZN = 16
OWN = CW // 64
TILE = 512
SUB = 16
CHUNK = 512


def dot_nn(a, b):
    return lax.dot_general(a, b, (((1,), (0,)), ((), ())), preferred_element_type=jnp.float32)


def dot_nt(a, b):
    return lax.dot_general(a, b, (((1,), (1,)), ((), ())), preferred_element_type=jnp.float32)


def dot_tn(a, b):
    return lax.dot_general(a, b, (((0,), (0,)), ((), ())), preferred_element_type=jnp.float32)


def remote(src, dst, ssem, rsem, dev):
    return pltpu.make_async_remote_copy(
        src_ref=src, dst_ref=dst, send_sem=ssem, recv_sem=rsem, device_id=dev, device_id_type=MESH
    )


def kernel(
    q_ref, k_ref, v_ref, g_ref, w_ref, kb_ref, kc_ref,
    dq_out, dk_out, dw_out,
    qg, kg, vg, gall, gturn, wbuf, wt, bias, work, expos, half, outs, wide, inverse, gheads, dqb, dkb,
    rsrc, r1, t1, r2, t2, r3,
    in_send, in_recv, loc, g_send, g_recv, w_send, w_recv, o_send, o_recv, r_send, r_recv,
):
    bf, f32 = jnp.bfloat16, jnp.float32
    dp = lax.axis_index("dp")
    me = lax.axis_index("seq")
    z = dp // 4
    quad = dp % 4
    xl = quad // 2
    core = quad % 2
    xh = me // 4
    y = me % 4

    def seq_at(dx, dy):
        return ((xh + dx) % 2) * 4 + (y + dy) % 4

    order = [(0, 0), (0, 3), (0, 1), (1, 0), (0, 2), (1, 3), (1, 1), (1, 2)]
    slot_of = {o: seq_at(*o) for o in order}
    peers = [slot_of[o] for o in order[1:]]
    mate = (z * 4 + xl * 2 + (1 - core), me)
    side = (z * 4 + (1 - xl) * 2 + core, me)
    along_z = [(((z + d) % ZN) * 4 + quad, me) for d in range(1, ZN)]

    barrier = pltpu.get_barrier_semaphore()
    targets = along_z + [(dp, p) for p in peers] + [mate, side]
    for t in targets:
        pl.semaphore_signal(barrier, inc=1, device_id=t, device_id_type=MESH)

    def cols(p, h):
        return pl.ds(pl.multiple_of(p * LW + h * HD, 128), HD)

    inputs = ((q_ref, qg), (k_ref, kg), (v_ref, vg))
    local = [pltpu.make_async_copy(g_ref, gall.at[me], loc.at[0])]
    local.append(pltpu.make_async_copy(w_ref, wbuf.at[quad, z], loc.at[1]))
    for a, (src, dst) in enumerate(inputs):
        for h in range(LH):
            local.append(pltpu.make_async_copy(src.at[:, cols(me, h)], dst.at[h, me], loc.at[2 + a * LH + h]))
    for c in local:
        c.start()

    key_block = lax.broadcasted_iota(jnp.int32, (NB, LEN), 1) // BLK
    entry = lax.broadcasted_iota(jnp.int32, (NB, 1), 0)
    lane = lax.broadcasted_iota(jnp.int32, (1, HEADS), 1)
    for h in range(LH):
        mine = lane == me * LH + h

        def mask_row(i, carry):
            count = jnp.sum(jnp.where(mine, kc_ref[pl.ds(i, 1), :], 0), axis=1, keepdims=True)
            listed = jnp.sum(jnp.where(mine, kb_ref[i], 0), axis=1, keepdims=True)
            listed = jnp.where(entry < count, listed, -1)
            hit = jnp.where(listed == key_block, 1.0, 0.0).astype(f32)
            found = jnp.max(hit, axis=0, keepdims=True)
            bias[h, i] = jnp.where(found > 0.5, 0.0, -jnp.inf).astype(f32)
            return carry

        lax.fori_loop(0, NB, mask_row, 0)

    pl.semaphore_wait(barrier, len(targets))

    up, down, across = (dp, seq_at(0, 1)), (dp, seq_at(0, 3)), (dp, seq_at(1, 0))

    def sem_of(dx, dy, part):
        return (order.index((dx % 2, dy % 4)) - 1) * 2 + part

    g_copies = {}

    def pass_on(dx, dy, part, way):
        dev, tdx, tdy = {"up": (up, dx, dy - 1), "down": (down, dx, dy + 1), "across": (across, dx + 1, dy)}[way]
        rows = pl.ds(part * HALF, HALF)
        n = sem_of(tdx, tdy, part)
        slot = slot_of[(dx % 2, dy % 4)]
        src = g_ref.at[rows] if (dx, dy) == (0, 0) else gall.at[slot, rows]
        c = remote(src, gall.at[slot, rows], g_send.at[n], g_recv.at[n], dev)
        c.start()
        g_copies[n] = c

    done = set()

    def arrived(dx, dy, part):
        n = sem_of(dx, dy, part)
        if n not in done:
            done.add(n)
            g_copies[n].wait_recv()

    for part in (0, 1):
        pass_on(0, 0, part, "across")
    pass_on(0, 0, 0, "up")
    pass_on(0, 0, 1, "down")
    pass_on(0, 0, 1, "up")
    pass_on(0, 0, 0, "down")

    w_copies = []
    for d in range(1, ZN):
        w_copies.append(remote(w_ref, wbuf.at[quad, z], w_send.at[d - 1], w_recv.at[d - 1], along_z[d - 1]))
    for c in w_copies:
        c.start()

    in_copies = []

    def send_inputs(h):
        for a, (src, dst) in enumerate(inputs):
            for i, p in enumerate(peers):
                n = (h * 3 + a) * 7 + i
                c = remote(src.at[:, cols(p, h)], dst.at[h, me], in_send.at[n], in_recv.at[n], (dp, p))
                c.start()
                in_copies.append(c)

    def turn(step):
        slot = slot_of[order[step]]
        place = pl.ds(pl.multiple_of(slot * ROWS, 128), ROWS)

        def piece(i, carry):
            cc = pl.ds(pl.multiple_of(i * CHUNK, 128), CHUNK)
            gturn[cc, place] = gall[slot, :, cc].T
            return carry

        lax.fori_loop(0, CW // CHUNK, piece, 0)

    def inputs_arrived(h):
        for c in in_copies[h * 21 : (h + 1) * 21]:
            c.wait_recv()

    def assemble(i, carry):
        group = jnp.concatenate([wbuf[q, i].astype(f32) for q in range(4)], axis=0)
        wt[pl.ds(pl.multiple_of(i * 4 * OWN, 32), 4 * OWN), :] = group.astype(bf)
        return carry

    far = (1 - xl) * 2 + core

    def head_gradients(column):
        first = column * 4
        part = dot_nn(gall[pl.ds(first, 4)].reshape(4 * ROWS, CW), wt[...]).astype(bf)
        rows = pl.ds(pl.multiple_of(first * ROWS, 4 * ROWS), 4 * ROWS)
        for h in range(LH):
            gheads[h, rows, :] = part[:, h * HD : (h + 1) * HD]

    scale = HD ** -0.5
    shards = TILE // ROWS

    def forward(h):
        key = kg[h].reshape(LEN, HD)

        def scores(i, carry):
            query = qg[h, pl.ds(i * shards, shards)].reshape(TILE, HD)
            work[pl.ds(pl.multiple_of(i * TILE, TILE), TILE), :] = dot_nt(query, key)
            return carry

        lax.fori_loop(0, LEN // TILE, scores, 0)

        def softmax(i, carry):
            mask = bias[h, i]
            for j in range(BLK // SUB):
                rows = pl.ds(pl.multiple_of(i * BLK + j * SUB, SUB), SUB)
                s = work[rows, :] * (scale * LOG2E) + mask
                expo = jnp.exp2(s - jnp.max(s, axis=-1, keepdims=True))
                inverse[h % 2, rows, :] = 1.0 / jnp.sum(expo, axis=-1, keepdims=True)
                expos[h % 2, rows, :] = expo
                half[rows, :] = expo.astype(bf)
            return carry

        lax.fori_loop(0, NB, softmax, 0)

        def mix(i, carry):
            rows = pl.ds(pl.multiple_of(i * TILE, TILE), TILE)
            part = dot_nn(half[rows, :], vg[h].reshape(LEN, HD)) * inverse[h % 2, rows, :]
            wide[h % 2, rows, :] = part
            outs[rows, h * HD : (h + 1) * HD] = part.astype(bf)
            return carry

        lax.fori_loop(0, LEN // TILE, mix, 0)

    def weight_gradient(first, count):
        group = CW // 4
        mine = slice(first * HD, (first + count) * HD)

        def product(i, carry):
            part = dot_nn(gturn[pl.ds(pl.multiple_of(i * group, 128), group), :], outs[:, mine])
            for n in range(count):
                one = part[:, n * HD : (n + 1) * HD].reshape(4, 4, OWN, HD).astype(bf)
                for q in range(4):
                    rsrc[first + n, q, pl.ds(i * 4, 4)] = one[:, q]
            return carry

        lax.fori_loop(0, 4, product, 0)

    pair, sides, zs = {}, {}, {}

    def sum_pair(h):
        pair[h] = [
            remote(
                rsrc.at[h, x * 2 + 1 - core], r1.at[h, x], r_send.at[h * 18 + x], r_recv.at[h * 18 + x], mate
            )
            for x in range(2)
        ]
        for c in pair[h]:
            c.start()

    def sum_side(h):
        for c in pair[h]:
            c.wait_recv()

        def add(i, carry):
            t1[h, i] = (rsrc[h, far, i].astype(f32) + r1[h, 1 - xl, i].astype(f32)).astype(bf)
            return carry

        lax.fori_loop(0, ZN, add, 0)
        sides[h] = remote(t1.at[h], r2.at[h], r_send.at[h * 18 + 2], r_recv.at[h * 18 + 2], side)
        sides[h].start()

    def sum_z(h):
        sides[h].wait_recv()

        def add(i, carry):
            t2[h, i] = (rsrc[h, quad, i].astype(f32) + r1[h, xl, i].astype(f32) + r2[h, i].astype(f32)).astype(bf)
            return carry

        lax.fori_loop(0, ZN, add, 0)
        zs[h] = []
        for d in range(1, ZN):
            n = h * 18 + 2 + d
            zs[h].append(
                remote(t2.at[h, (z + d) % ZN], r3.at[h, d - 1], r_send.at[n], r_recv.at[n], along_z[d - 1])
            )
        for c in zs[h]:
            c.start()

    def sum_last(h):
        total = t2[h, z].astype(f32)
        for d, c in enumerate(zs[h]):
            c.wait_recv()
            total = total + r3[h, d].astype(f32)
        dw_out[:, h * HD : (h + 1) * HD] = total

    o_copies = []

    def send_back(h, a, src, dst):
        c = pltpu.make_async_copy(src.at[h, me], dst.at[:, cols(me, h)], loc.at[11 + h * 2 + a])
        c.start()
        o_copies.append((True, c))
        for i, p in enumerate(peers):
            n = (h * 2 + a) * 7 + i
            c = remote(src.at[h, p], dst.at[:, cols(me, h)], o_send.at[n], o_recv.at[n], (dp, p))
            c.start()
            o_copies.append((False, c))

    def backward(h, between):
        key = kg[h].reshape(LEN, HD)
        value = vg[h].reshape(LEN, HD)

        def products(i, carry):
            rows = pl.ds(pl.multiple_of(i * TILE, TILE), TILE)
            work[rows, :] = dot_nt(gheads[h, rows, :], value)
            return carry

        lax.fori_loop(0, LEN // TILE, products, 0)
        between()

        def softmax_grad(i, carry):
            for j in range(BLK // SUB):
                rows = pl.ds(pl.multiple_of(i * BLK + j * SUB, SUB), SUB)
                delta = jnp.sum(wide[h % 2, rows, :] * gheads[h, rows, :].astype(f32), axis=-1, keepdims=True)
                factor = inverse[h % 2, rows, :] * scale
                half[rows, :] = (expos[h % 2, rows, :] * ((work[rows, :] - delta) * factor)).astype(bf)
            return carry

        lax.fori_loop(0, NB, softmax_grad, 0)

        def query_grad(i, carry):
            rows = pl.ds(pl.multiple_of(i * TILE, TILE), TILE)
            part = dot_nn(half[rows, :], key).astype(bf)
            dqb[h, pl.ds(i * shards, shards)] = part.reshape(shards, ROWS, HD)
            return carry

        lax.fori_loop(0, LEN // TILE, query_grad, 0)
        send_back(h, 0, dqb, dq_out)

        def key_grad(i, carry):
            rows = pl.ds(pl.multiple_of(i * TILE, TILE), TILE)
            part = dot_tn(half[:, rows], qg[h].reshape(LEN, HD)).astype(bf)
            dkb[h, pl.ds(i * shards, shards)] = part.reshape(shards, ROWS, HD)
            return carry

        lax.fori_loop(0, LEN // TILE, key_grad, 0)
        send_back(h, 1, dkb, dk_out)

    send_inputs(0)
    send_inputs(1)
    arrived(0, 3, 0)
    pass_on(0, 3, 0, "up")
    pass_on(0, 3, 0, "across")
    arrived(0, 1, 1)
    pass_on(0, 1, 1, "down")
    pass_on(0, 1, 1, "across")
    arrived(1, 0, 0)
    pass_on(1, 0, 0, "down")
    arrived(1, 0, 1)
    pass_on(1, 0, 1, "up")
    for c in local:
        c.wait()
    turn(0)
    inputs_arrived(0)
    forward(0)

    for c in w_copies:
        c.wait_recv()
    plane = [
        remote(wbuf.at[quad], wbuf.at[quad], w_send.at[15], w_recv.at[15], mate),
        remote(wbuf.at[quad], wbuf.at[quad], w_send.at[16], w_recv.at[16], side),
    ]
    for c in plane:
        c.start()
    inputs_arrived(1)
    forward(1)
    arrived(1, 3, 0)
    pass_on(1, 3, 0, "up")
    arrived(1, 1, 1)
    pass_on(1, 1, 1, "down")
    send_inputs(2)
    for step in range(1, 5):
        for part in (0, 1):
            arrived(*order[step], part)
        turn(step)
    plane[1].wait_recv()
    plane.append(remote(wbuf.at[far], wbuf.at[far], w_send.at[17], w_recv.at[17], mate))
    plane[2].start()
    plane[0].wait_recv()
    plane[2].wait_recv()
    lax.fori_loop(0, ZN, assemble, 0)
    head_gradients(xh)
    for step in range(5, SEQ):
        for part in (0, 1):
            arrived(*order[step], part)
        turn(step)
    weight_gradient(0, 2)
    sum_pair(0)
    sum_pair(1)
    head_gradients(1 - xh)
    sum_side(0)
    sum_side(1)
    backward(0, lambda: None)
    inputs_arrived(2)
    sum_z(0)
    forward(2)
    sum_z(1)
    weight_gradient(2, 1)
    sum_pair(2)
    backward(1, lambda: sum_side(2))
    backward(2, lambda: sum_z(2))
    sum_last(0)
    sum_last(1)
    sum_last(2)

    for here, c in o_copies:
        c.wait()
    for c in in_copies + w_copies + plane + list(g_copies.values()):
        c.wait_send()
    for h in range(LH):
        for c in pair[h] + [sides[h]] + zs[h]:
            c.wait_send()


def per_device(queries, key_states, value_states, grad_out, out_weight, key_blocks, key_count):
    bf, f32 = jnp.bfloat16, jnp.float32
    vmem = pl.BlockSpec(memory_space=pltpu.VMEM)
    dma = pltpu.SemaphoreType.DMA
    head_rows = pltpu.VMEM((LH, SEQ, ROWS, HD), bf)
    grad_q, grad_k, grad_w = pl.pallas_call(
        kernel,
        name="bigbird_backward",
        out_shape=(
            jax.ShapeDtypeStruct((ROWS, HEADS * HD), bf),
            jax.ShapeDtypeStruct((ROWS, HEADS * HD), bf),
            jax.ShapeDtypeStruct((OWN, LW), f32),
        ),
        in_specs=[vmem] * 7,
        out_specs=(vmem, vmem, vmem),
        scratch_shapes=[
            head_rows, head_rows, head_rows,
            pltpu.VMEM((SEQ, ROWS, CW), bf),
            pltpu.VMEM((CW, LEN), bf),
            pltpu.VMEM((4, ZN, OWN, LW), bf),
            pltpu.VMEM((CW, LW), bf),
            pltpu.VMEM((LH, NB, 1, LEN), f32),
            pltpu.VMEM((LEN, LEN), f32),
            pltpu.VMEM((2, LEN, LEN), f32),
            pltpu.VMEM((LEN, LEN), bf),
            pltpu.VMEM((LEN, LW), bf),
            pltpu.VMEM((2, LEN, HD), f32),
            pltpu.VMEM((2, LEN, 1), f32),
            pltpu.VMEM((LH, LEN, HD), bf),
            head_rows, head_rows,
            pltpu.VMEM((LH, 4, ZN, OWN, HD), bf),
            pltpu.VMEM((LH, 2, ZN, OWN, HD), bf),
            pltpu.VMEM((LH, ZN, OWN, HD), bf),
            pltpu.VMEM((LH, ZN, OWN, HD), bf),
            pltpu.VMEM((LH, ZN, OWN, HD), bf),
            pltpu.VMEM((LH, ZN - 1, OWN, HD), bf),
            dma((63,)), dma((63,)), dma((17,)),
            dma((14,)), dma((14,)),
            dma((18,)), dma((18,)),
            dma((42,)), dma((42,)),
            dma((54,)), dma((54,)),
        ],
        compiler_params=pltpu.CompilerParams(
            collective_id=0, has_side_effects=True, vmem_limit_bytes=60 * 1024 * 1024
        ),
    )(queries, key_states, value_states, grad_out, out_weight.T, key_blocks.transpose(1, 2, 0), key_count.T)
    return grad_q, grad_k, grad_w.T


def solution(mesh):
    return jax.shard_map(
        per_device,
        mesh=mesh,
        in_specs=(
            P(("dp", "seq"), None),
            P(("dp", "seq"), None),
            P(("dp", "seq"), None),
            P(("dp", "seq"), None),
            P("seq", "dp"),
            P(),
            P(),
        ),
        out_specs=(P(("dp", "seq"), None), P(("dp", "seq"), None), P("seq", "dp")),
        check_vma=False,
    )
```
